256 devices in a mesh: member: 2 (over x_lo), space: 128 (over z, y, x_hi, core).
Axes of the slice: x: 4 (x_hi: 2, x_lo: 2; x = x_hi * 2 + x_lo), y: 4, z: 8, core: 2. Of those that a mesh axis runs over, the one named last changes fastest.
Arguments:
- params: float32 [256, 512, 1024], P('member', 'space'), may hold values from -2 to 2
- state: float32 [256, 512, 1024], P('member', 'space'), may hold values from -6 to 6
- regime: int32 [512, 1024], P('space'), may hold values from 0 to 7
- regime_coefs: float32 [8, 4], replicated, may hold values from 0.1 to 0.5
- observation_index: int32 [65536], P('space'), may hold values from 0 to 524287, as said below
- measured_values: float32 [65536], P('space'), may hold values from -6 to 6
- observation_spread: float32 [65536], P('space'), may hold values from 0.1 to 1
- observation_jitter: float32 [256, 65536], P('member', 'space'), may hold values from -6 to 6
Outputs:
- revised_log_diffusivity: float32 [256, 512, 1024], P('member', 'space')
- predicted_member_state: float32 [256, 512, 1024], P('member', 'space')
The draws below stay inside these ranges and needn't reach their ends.
Inputs may be any that keep to these rules, and one draw needn't show every extreme that they name: `observation_index`: observation o lies in the strip of rows o // 512 * 4 up to (o // 512 + 1) * 4 - 1; the first observation of each strip sits on its first cell, the second on its last cell; cells may repeat.
All inputs are finite; a program needn't handle non-finite values.
Results may differ from the reference program's by a relative error of at most 0.015.
Values sent between devices are 32-bit elements; how exact they have to be, the bound alone decides.
No kernel may reach another device: no remote copies, remote signals or barrier semaphores. Data moves between devices by JAX's collectives and lax.ppermute only.
A program may use at most 64 MiB of HBM per device.

```python
import math
import jax
import jax.numpy as jnp
from jax import lax

ROWS_DEV = 4
NCOLS = 1024
OBS_DEV = 512
REGIMES = 8
MEMBERS = 256
NROWS = 512
NOBS = 65536


def draw_observation_index(key, part):
    strip_cells = ROWS_DEV * NCOLS
    order = jnp.arange(NOBS, dtype=jnp.int32)
    strip = order // OBS_DEV
    position = order % OBS_DEV
    local_cell = jax.random.randint(key, (NOBS,), 0, strip_cells, dtype=jnp.int32)
    local_cell = jnp.where(position == 0, 0, jnp.where(position == 1, strip_cells - 1, local_cell))
    return (strip * strip_cells + local_cell).astype(jnp.int32)


def place_ends(drawn, stream_key, low, top_value):
    extent = drawn.shape
    spot = [jax.random.randint(jax.random.fold_in(stream_key, axis), (), 0, extent[axis]) for axis in range(len(extent))]
    drawn = drawn.at[tuple(spot)].set(low)
    longest = extent.index(max(extent))
    spot[longest] = (spot[longest] + 1) % extent[longest]
    return drawn.at[tuple(spot)].set(top_value)


def shard_levels(key, dims, split, low, top_value):
    gain, own = 1.0, jax.random.fold_in(key, 6)
    for dim, shards_of in split:
        steps = jnp.exp(jax.random.uniform(jax.random.fold_in(own, dim), (shards_of,), jnp.float32, low / len(split), top_value / len(split)))
        gain = gain * jnp.repeat(steps, dims[dim] // shards_of).reshape([-1 if axis == dim else 1 for axis in range(len(dims))])
    return gain


def scatter_about(rng, dims, width, reach, split=(), held_as=jnp.bfloat16):
    result = jax.random.normal(rng, dims, jnp.float32) * width
    if len(split) > 0:
        result = shard_levels(rng, dims, split, -0.22, 0.18) * result
    return jnp.clip(result, min=-reach, max=reach).astype(held_as)


def setup_inputs(seed: int = 0) -> dict:
    splits = jax.random.split(jax.random.key(seed), 9)
    params = scatter_about(splits[0], (MEMBERS, NROWS, NCOLS), 0.5, 2.0, ((0, 2), (1, 128)), jnp.float32)
    state = scatter_about(splits[1], (MEMBERS, NROWS, NCOLS), 1.0, 6.0, ((0, 2), (1, 128)), jnp.float32)
    regime = place_ends(jax.random.randint(splits[2], (NROWS, NCOLS), 0, REGIMES), jax.random.fold_in(splits[2], 1), 0, REGIMES - 1).astype(jnp.int32)
    regime_coefs = jnp.clip(jax.random.uniform(splits[3], (REGIMES, 4), jnp.float32, 0.1, 0.5), 0.1, 0.5)
    observation_index = draw_observation_index(jax.random.fold_in(splits[8], 71), 0)
    measured_values = scatter_about(splits[5], (NOBS,), 1.0, 6.0, ((0, 128),), jnp.float32)
    observation_spread = jnp.clip(jnp.exp(math.log(1.0) - 2.3025851 * jax.random.uniform(splits[6], (NOBS,), jnp.float32) ** shard_levels(splits[6], (NOBS,), ((0, 128),), -0.2, 0.2)), 0.1, 1.0)
    observation_jitter = scatter_about(splits[7], (MEMBERS, NOBS), 1.0, 6.0, ((0, 2), (1, 128)), jnp.float32)
    return {"params": params, "state": state, "regime": regime, "regime_coefs": regime_coefs, "observation_index": observation_index, "measured_values": measured_values, "observation_spread": observation_spread, "observation_jitter": observation_jitter}


time_step = 0.06

def coef_fields(regime, regime_coefs):
    levels = jnp.arange(regime_coefs.shape[0], dtype=jnp.int32)
    onehot = (regime[None, :, :] == levels[:, None, None]).astype(jnp.float32)
    return jnp.einsum('rd,rxy->dxy', regime_coefs, onehot, precision=lax.Precision.HIGHEST)

def advance(extended, rates, coefs):
    center = extended[..., 1:-1, :]
    widths = [(0, 0)] * (center.ndim - 1) + [(1, 1)]
    padded_cols = jnp.pad(center, widths)
    above = extended[..., :-2, :]
    below = extended[..., 2:, :]
    left_side = padded_cols[..., :-2]
    right_side = padded_cols[..., 2:]
    flow = coefs[0] * (above - center) + coefs[1] * (below - center)
    flow = flow + coefs[2] * (left_side - center) + coefs[3] * (right_side - center)
    return center + rates * flow

def reference(params, state, regime, regime_coefs, observation_index, measured_values, observation_spread, observation_jitter):
    coefs = coef_fields(regime, regime_coefs)

    def single_member(pair):
        member_params, member_state = pair
        rates = time_step * jnp.exp(member_params)
        current = member_state
        for repeat in range(2):
            current = advance(jnp.pad(current, ((1, 1), (0, 0))), rates, coefs)
        return current
    predicted_member_state = lax.map(single_member, (params, state))
    member_list = params.shape[0]
    square_root_scale = math.sqrt(member_list - 1)
    flattened_grid = predicted_member_state.reshape(member_list, -1)
    predicted_fields = jnp.take(flattened_grid, observation_index, axis=1)
    ensemble_mean_prediction = lax.optimization_barrier(jnp.sum(predicted_fields, axis=0)) / member_list
    member_departures = (predicted_fields - ensemble_mean_prediction[None, :]) / (observation_spread[None, :] * square_root_scale)
    observation_misfits = (measured_values[None, :] + observation_spread[None, :] * observation_jitter - predicted_fields) / observation_spread[None, :]
    stacked = jnp.concatenate([member_departures, observation_misfits], axis=0)
    gram_full = jnp.dot(member_departures.astype(jnp.float32), stacked.T.astype(jnp.float32), precision=lax.Precision.HIGHEST, preferred_element_type=jnp.float32)
    gram = gram_full[:, :member_list]
    cross = gram_full[:, member_list:]
    system = jnp.eye(member_list, dtype=jnp.float32) + gram
    factor = jnp.linalg.cholesky(system)
    mixing = jax.scipy.linalg.cho_solve((factor, True), cross)
    param_anom = params / square_root_scale
    update = jnp.einsum('kj,kxy->jxy', mixing, param_anom, precision=lax.Precision.HIGHEST)
    revised_log_diffusivity = params + update
    return (revised_log_diffusivity, predicted_member_state)
```

```python
import math

import jax
import jax.numpy as jnp
from jax import lax
from jax.sharding import Mesh, PartitionSpec as P

time_step = 0.06
SPACE = ("z", "y", "xh", "core")
CHIPS = ("z", "y", "xh")
SWAP = [(0, 1), (1, 0)]


def coef_fields(regime, regime_coefs):
    levels = jnp.arange(regime_coefs.shape[0], dtype=jnp.int32)
    onehot = (regime[None, :, :] == levels[:, None, None]).astype(jnp.float32)
    return jnp.einsum("rd,rxy->dxy", regime_coefs, onehot, precision=lax.Precision.HIGHEST)


def with_halo(cells):
    count = lax.axis_size(SPACE)
    ends = count - 1
    head = cells[:, :1]
    tail = cells[:, -1:]
    above = lax.ppermute(tail, SPACE, [(i, i + 1) for i in range(ends)])
    below = lax.ppermute(head, SPACE, [(i + 1, i) for i in range(ends)])
    return jnp.concatenate([above, cells, below], axis=1)


def advance(extended, rates, coefs):
    center = extended[..., 1:-1, :]
    widths = [(0, 0)] * (center.ndim - 1) + [(1, 1)]
    padded_cols = jnp.pad(center, widths)
    above = extended[..., :-2, :]
    below = extended[..., 2:, :]
    left_side = padded_cols[..., :-2]
    right_side = padded_cols[..., 2:]
    flow = coefs[0] * (above - center) + coefs[1] * (below - center)
    flow = flow + coefs[2] * (left_side - center) + coefs[3] * (right_side - center)
    return center + rates * flow


def reduce_over_space(block):
    half = block.shape[0] // 2
    core = lax.axis_index("core")
    low, high = block[:half], block[half:]
    first = core == 0
    kept = jnp.where(first, low, high)
    sent = jnp.where(first, high, low)
    part = kept + lax.ppermute(sent, "core", SWAP)
    chips = lax.axis_size(CHIPS)
    pieces = lax.all_to_all(part, CHIPS, 0, 0, tiled=True)
    piece = jnp.sum(pieces.reshape(chips, half // chips, -1), axis=0)
    spread = jnp.broadcast_to(piece[None], (chips,) + piece.shape).reshape(half, -1)
    summed = lax.all_to_all(spread, CHIPS, 0, 0, tiled=True)
    other = lax.ppermute(summed, "core", SWAP)
    return jnp.concatenate(
        [jnp.where(first, summed, other), jnp.where(first, other, summed)], axis=0
    )


def body(
    params,
    state,
    regime,
    regime_coefs,
    observation_index,
    measured_values,
    observation_spread,
    observation_jitter,
):
    own = params.shape[0]
    strip_rows = params.shape[1]
    columns = params.shape[2]
    members = own * lax.axis_size("member")
    square_root_scale = math.sqrt(members - 1)
    coefs = coef_fields(regime, regime_coefs)
    rates = time_step * jnp.exp(params)
    current = state
    for repeat in range(2):
        current = advance(with_halo(current), rates, coefs)
    local_index = observation_index - lax.axis_index(SPACE) * (strip_rows * columns)
    flat = current.reshape(own, strip_rows * columns)
    mine = jnp.take(flat, local_index, axis=1)
    theirs = lax.ppermute(mine, "member", SWAP)
    params_there, theirs2 = lax.optimization_barrier((params, theirs))
    other_params = lax.ppermute(params_there, "member", SWAP)
    predicted = jnp.concatenate([mine, theirs2], axis=0)
    mean = jnp.sum(predicted, axis=0) / members
    anomalies = (predicted - mean[None, :]) / (observation_spread[None, :] * square_root_scale)
    innovations = (
        measured_values[None, :] + observation_spread[None, :] * observation_jitter - mine
    ) / observation_spread[None, :]
    stacked = jnp.concatenate([anomalies, innovations], axis=0)
    rows = jnp.dot(
        anomalies, stacked.T, precision=lax.Precision.HIGHEST, preferred_element_type=jnp.float32
    )
    total = reduce_over_space(rows)
    gram = total[:, :members]
    cross = total[:, members:]
    system = jnp.eye(members, dtype=jnp.float32) + gram
    factor = jnp.linalg.cholesky(system)
    mixing = jax.scipy.linalg.cho_solve((factor, True), cross)
    both = jnp.concatenate([params, other_params], axis=0) / square_root_scale
    update = jnp.einsum("kj,kxy->jxy", mixing, both, precision=lax.Precision.HIGHEST)
    return (params + update, current)


def solution(mesh):
    fine = Mesh(mesh.devices.reshape(2, 8, 4, 2, 2), ("member",) + SPACE)
    in_specs = (
        P("member", SPACE, None),
        P("member", SPACE, None),
        P(SPACE, None),
        P(),
        P(SPACE),
        P(SPACE),
        P(SPACE),
        P("member", SPACE),
    )
    out_specs = (P("member", SPACE, None), P("member", SPACE, None))
    return jax.shard_map(body, mesh=fine, in_specs=in_specs, out_specs=out_specs, check_vma=False)
```

```python
import math

import jax
import jax.numpy as jnp
from jax import lax
from jax.experimental import pallas as pl
from jax.experimental.pallas import tpu as pltpu
from jax.sharding import Mesh, PartitionSpec as P

time_step = 0.06
SPACE = ("z", "y", "xh", "core")
CHIPS = ("z", "y", "xh")
SWAP = [(0, 1), (1, 0)]
HIGHEST = lax.Precision.HIGHEST
BLOCK = 64


def invert_block(block):
    size = block.shape[0]
    wide = 2 * size
    row_id = lax.broadcasted_iota(jnp.int32, (size, wide), 0)
    r = lax.broadcasted_iota(jnp.int32, (size, size), 0)
    c = lax.broadcasted_iota(jnp.int32, (size, size), 1)
    aug = jnp.concatenate([block, (r == c).astype(jnp.float32)], axis=1)
    for p in range(0, size, 4):
        cols = [jnp.broadcast_to(aug[:, p + i : p + i + 1], (size, wide)) for i in range(4)]
        rows = [aug[p + i : p + i + 1, :] for i in range(4)]
        e = [[cols[j][p + i : p + i + 1, :] for j in range(4)] for i in range(4)]
        a, b, d = e[0][0], e[1][0], e[1][1]
        inv = 1.0 / (a * d - b * b)
        t0 = (d * rows[0] - b * rows[1]) * inv
        t1 = (a * rows[1] - b * rows[0]) * inv
        u, v, w, x = e[2][0], e[2][1], e[3][0], e[3][1]
        l00 = (d * u - b * v) * inv
        l01 = (a * v - b * u) * inv
        l10 = (d * w - b * x) * inv
        l11 = (a * x - b * w) * inv
        sa = e[2][2] - (u * l00 + v * l01)
        sb = e[3][2] - (w * l00 + x * l01)
        sd = e[3][3] - (w * l10 + x * l11)
        s2 = rows[2] - (l00 * rows[0] + l01 * rows[1])
        s3 = rows[3] - (l10 * rows[0] + l11 * rows[1])
        sinv = 1.0 / (sa * sd - sb * sb)
        n2 = (sd * s2 - sb * s3) * sinv
        n3 = (sa * s3 - sb * s2) * sinv
        news = [t0 - (l00 * n2 + l10 * n3), t1 - (l01 * n2 + l11 * n3), n2, n3]
        out = aug
        for i in range(4):
            out = out - cols[i] * news[i]
        for i in range(4):
            out = jnp.where(row_id == p + i, news[i], out)
        aug = out
    return aug[:, size:]


def solve_kernel(g_ref, x_ref, w):
    m = g_ref.shape[0]
    w[...] = g_ref[...]
    r = lax.broadcasted_iota(jnp.int32, (m, m), 0)
    c = lax.broadcasted_iota(jnp.int32, (m, m), 1)
    w[:, :m] = w[:, :m] + (r == c).astype(jnp.float32)
    rows = lax.broadcasted_iota(jnp.int32, (m, 1), 0)
    for at in range(0, m, BLOCK):
        end = at + BLOCK
        lo = end // 128 * 128
        inv = invert_block(w[at:end, at:end])
        new = jnp.dot(inv, w[at:end, lo:], precision=HIGHEST, preferred_element_type=jnp.float32)
        left = jnp.where((rows >= at) & (rows < end), 0.0, w[:, at:end])
        w[:, lo:] = w[:, lo:] - jnp.dot(
            left, new, precision=HIGHEST, preferred_element_type=jnp.float32
        )
        w[at:end, lo:] = new
    x_ref[...] = w[:, m:]


def solve(system):
    m, wide = system.shape
    vmem = pl.BlockSpec(memory_space=pltpu.VMEM)
    return pl.pallas_call(
        solve_kernel,
        out_shape=jax.ShapeDtypeStruct((m, wide - m), jnp.float32),
        in_specs=[vmem],
        out_specs=vmem,
        scratch_shapes=[pltpu.VMEM((m, wide), jnp.float32)],
        cost_estimate=pl.CostEstimate(flops=200_000_000, bytes_accessed=600_000, transcendentals=0),
        name="solve",
    )(system)


def coef_fields(regime, regime_coefs):
    levels = jnp.arange(regime_coefs.shape[0], dtype=jnp.int32)
    onehot = (regime[None, :, :] == levels[:, None, None]).astype(jnp.float32)
    return jnp.einsum("rd,rxy->dxy", regime_coefs, onehot, precision=lax.Precision.HIGHEST)


def with_halo(cells):
    count = lax.axis_size(SPACE)
    ends = count - 1
    head = cells[:, :1]
    tail = cells[:, -1:]
    above = lax.ppermute(tail, SPACE, [(i, i + 1) for i in range(ends)])
    below = lax.ppermute(head, SPACE, [(i + 1, i) for i in range(ends)])
    return jnp.concatenate([above, cells, below], axis=1)


def advance(extended, rates, coefs):
    center = extended[..., 1:-1, :]
    widths = [(0, 0)] * (center.ndim - 1) + [(1, 1)]
    padded_cols = jnp.pad(center, widths)
    above = extended[..., :-2, :]
    below = extended[..., 2:, :]
    left_side = padded_cols[..., :-2]
    right_side = padded_cols[..., 2:]
    flow = coefs[0] * (above - center) + coefs[1] * (below - center)
    flow = flow + coefs[2] * (left_side - center) + coefs[3] * (right_side - center)
    return center + rates * flow


def reduce_over_space(block):
    half = block.shape[0] // 2
    core = lax.axis_index("core")
    low, high = block[:half], block[half:]
    first = core == 0
    kept = jnp.where(first, low, high)
    sent = jnp.where(first, high, low)
    part = kept + lax.ppermute(sent, "core", SWAP)
    chips = lax.axis_size(CHIPS)
    pieces = lax.all_to_all(part, CHIPS, 0, 0, tiled=True)
    piece = jnp.sum(pieces.reshape(chips, half // chips, -1), axis=0)
    spread = jnp.broadcast_to(piece[None], (chips,) + piece.shape).reshape(half, -1)
    summed = lax.all_to_all(spread, CHIPS, 0, 0, tiled=True)
    other = lax.ppermute(summed, "core", SWAP)
    return jnp.concatenate(
        [jnp.where(first, summed, other), jnp.where(first, other, summed)], axis=0
    )


def strip(
    params,
    state,
    regime,
    regime_coefs,
    observation_index,
    measured_values,
    observation_spread,
    observation_jitter,
):
    own = params.shape[0]
    strip_rows = params.shape[1]
    columns = params.shape[2]
    members = own * lax.axis_size("member")
    square_root_scale = math.sqrt(members - 1)
    coefs = coef_fields(regime, regime_coefs)
    rates = time_step * jnp.exp(params)
    current = state
    for _ in range(2):
        current = advance(with_halo(current), rates, coefs)
    local_index = observation_index - lax.axis_index(SPACE) * (strip_rows * columns)
    flat = current.reshape(own, strip_rows * columns)
    mine = jnp.take(flat, local_index, axis=1)
    theirs = lax.ppermute(mine, "member", SWAP)
    params_there, theirs2 = lax.optimization_barrier((params, theirs))
    other_params = lax.ppermute(params_there, "member", SWAP)
    predicted = jnp.concatenate([mine, theirs2], axis=0)
    mean = jnp.sum(predicted, axis=0) / members
    anomalies = (predicted - mean[None, :]) / (observation_spread[None, :] * square_root_scale)
    innovations = (
        measured_values[None, :] + observation_spread[None, :] * observation_jitter - mine
    ) / observation_spread[None, :]
    stacked = jnp.concatenate([anomalies, innovations], axis=0)
    rows = jnp.dot(
        anomalies, stacked.T, precision=HIGHEST, preferred_element_type=jnp.float32
    )
    mixing = solve(reduce_over_space(rows))
    both = jnp.concatenate([params, other_params], axis=0) / square_root_scale
    update = jnp.einsum("kj,kxy->jxy", mixing, both, precision=lax.Precision.HIGHEST)
    return (params + update, current)


def solution(mesh):
    fine = Mesh(mesh.devices.reshape(2, 8, 4, 2, 2), ("member",) + SPACE)
    in_specs = (
        P("member", SPACE, None),
        P("member", SPACE, None),
        P(SPACE, None),
        P(),
        P(SPACE),
        P(SPACE),
        P(SPACE),
        P("member", SPACE),
    )
    out_specs = (P("member", SPACE, None), P("member", SPACE, None))
    return jax.shard_map(strip, mesh=fine, in_specs=in_specs, out_specs=out_specs, check_vma=False)
```

```python
import math

import jax
import jax.numpy as jnp
from jax import lax
from jax.experimental import pallas as pl
from jax.experimental.pallas import tpu as pltpu
from jax.sharding import Mesh, PartitionSpec as P

time_step = 0.06
SPACE = ("z", "y", "xh", "core")
CHIPS = ("z", "y", "xh")
SWAP = [(0, 1), (1, 0)]
HIGHEST = lax.Precision.HIGHEST
BLOCK = 64


def invert_block(block):
    size = block.shape[0]
    wide = 2 * size
    row_id = lax.broadcasted_iota(jnp.int32, (size, wide), 0)
    r = lax.broadcasted_iota(jnp.int32, (size, size), 0)
    c = lax.broadcasted_iota(jnp.int32, (size, size), 1)
    aug = jnp.concatenate([block, (r == c).astype(jnp.float32)], axis=1)
    for p in range(0, size, 4):
        cols = [jnp.broadcast_to(aug[:, p + i : p + i + 1], (size, wide)) for i in range(4)]
        rows = [aug[p + i : p + i + 1, :] for i in range(4)]
        e = [[cols[j][p + i : p + i + 1, :] for j in range(4)] for i in range(4)]
        a, b, d = e[0][0], e[1][0], e[1][1]
        inv = 1.0 / (a * d - b * b)
        t0 = (d * rows[0] - b * rows[1]) * inv
        t1 = (a * rows[1] - b * rows[0]) * inv
        u, v, w, x = e[2][0], e[2][1], e[3][0], e[3][1]
        l00 = (d * u - b * v) * inv
        l01 = (a * v - b * u) * inv
        l10 = (d * w - b * x) * inv
        l11 = (a * x - b * w) * inv
        sa = e[2][2] - (u * l00 + v * l01)
        sb = e[3][2] - (w * l00 + x * l01)
        sd = e[3][3] - (w * l10 + x * l11)
        s2 = rows[2] - (l00 * rows[0] + l01 * rows[1])
        s3 = rows[3] - (l10 * rows[0] + l11 * rows[1])
        sinv = 1.0 / (sa * sd - sb * sb)
        n2 = (sd * s2 - sb * s3) * sinv
        n3 = (sa * s3 - sb * s2) * sinv
        news = [t0 - (l00 * n2 + l10 * n3), t1 - (l01 * n2 + l11 * n3), n2, n3]
        out = aug
        for i in range(4):
            out = out - cols[i] * news[i]
        for i in range(4):
            out = jnp.where(row_id == p + i, news[i], out)
        aug = out
    return aug[:, size:]


def solve_kernel(g_ref, x_ref, w):
    m = g_ref.shape[0]
    w[...] = g_ref[...]
    r = lax.broadcasted_iota(jnp.int32, (m, m), 0)
    c = lax.broadcasted_iota(jnp.int32, (m, m), 1)
    w[:, :m] = w[:, :m] + (r == c).astype(jnp.float32)
    rows = lax.broadcasted_iota(jnp.int32, (m, 1), 0)
    for at in range(0, m, BLOCK):
        end = at + BLOCK
        lo = end // 128 * 128
        inv = invert_block(w[at:end, at:end])
        new = jnp.dot(inv, w[at:end, lo:], precision=HIGHEST, preferred_element_type=jnp.float32)
        left = jnp.where((rows >= at) & (rows < end), 0.0, w[:, at:end])
        w[:, lo:] = w[:, lo:] - jnp.dot(
            left, new, precision=HIGHEST, preferred_element_type=jnp.float32
        )
        w[at:end, lo:] = new
    x_ref[...] = w[:, m:]


def solve(system):
    m, wide = system.shape
    vmem = pl.BlockSpec(memory_space=pltpu.VMEM)
    return pl.pallas_call(
        solve_kernel,
        out_shape=jax.ShapeDtypeStruct((m, wide - m), jnp.float32),
        in_specs=[vmem],
        out_specs=vmem,
        scratch_shapes=[pltpu.VMEM((m, wide), jnp.float32)],
        cost_estimate=pl.CostEstimate(flops=200_000_000, bytes_accessed=600_000, transcendentals=0),
        name="solve",
    )(system)


def coef_fields(regime, regime_coefs):
    levels = jnp.arange(regime_coefs.shape[0], dtype=jnp.int32)
    onehot = (regime[None, :, :] == levels[:, None, None]).astype(jnp.float32)
    return jnp.einsum("rd,rxy->dxy", regime_coefs, onehot, precision=lax.Precision.HIGHEST)


def halo(head, tail):
    ends = lax.axis_size(SPACE) - 1
    above = lax.ppermute(tail, SPACE, [(i, i + 1) for i in range(ends)])
    below = lax.ppermute(head, SPACE, [(i + 1, i) for i in range(ends)])
    return above, below


def advance(above, center, below, rate, coef):
    padded = jnp.pad(center, ((0, 0), (1, 1)))
    flow = coef[0] * (above - center) + coef[1] * (below - center)
    flow = flow + coef[2] * (padded[:, :-2] - center) + coef[3] * (padded[:, 2:] - center)
    return center + rate * flow


def two_steps(rows, rates, coefs):
    last = len(rows) - 1
    above, below = halo(rows[0], rows[last])
    for repeat in range(2):
        ends = (
            advance(above, rows[0], rows[1], rates[0], coefs[0]),
            advance(rows[last - 1], rows[last], below, rates[last], coefs[last]),
        )
        inner = [
            advance(rows[r - 1], rows[r], rows[r + 1], rates[r], coefs[r]) for r in range(1, last)
        ]
        if repeat == 0:
            ends = lax.optimization_barrier(ends)
            above, below = halo(*ends)
        rows = [ends[0], *inner, ends[1]]
    return rows, below


def reduce_over_space(block):
    half = block.shape[0] // 2
    core = lax.axis_index("core")
    low, high = block[:half], block[half:]
    first = core == 0
    kept = jnp.where(first, low, high)
    sent = jnp.where(first, high, low)
    part = kept + lax.ppermute(sent, "core", SWAP)
    chips = lax.axis_size(CHIPS)
    pieces = lax.all_to_all(part, CHIPS, 0, 0, tiled=True)
    piece = jnp.sum(pieces.reshape(chips, half // chips, -1), axis=0)
    spread = jnp.broadcast_to(piece[None], (chips,) + piece.shape).reshape(half, -1)
    summed = lax.all_to_all(spread, CHIPS, 0, 0, tiled=True)
    other = lax.ppermute(summed, "core", SWAP)
    whole = jnp.concatenate(
        [jnp.where(first, summed, other), jnp.where(first, other, summed)], axis=0
    )
    return whole, summed


def strip(
    params,
    state,
    regime,
    regime_coefs,
    observation_index,
    measured_values,
    observation_spread,
    observation_jitter,
):
    own = params.shape[0]
    strip_rows = params.shape[1]
    columns = params.shape[2]
    members = own * lax.axis_size("member")
    square_root_scale = math.sqrt(members - 1)
    fields = coef_fields(regime, regime_coefs)
    coefs = [fields[:, r] for r in range(strip_rows)]
    by_row = lax.optimization_barrier(jnp.swapaxes(params, 0, 1))
    state_rows = lax.optimization_barrier(jnp.swapaxes(state, 0, 1))
    own_rows = [by_row[r] for r in range(strip_rows)]
    rates = [time_step * jnp.exp(row) for row in own_rows]
    rows, edge = two_steps([state_rows[r] for r in range(strip_rows)], rates, coefs)

    def swap(row, after):
        row, after = lax.optimization_barrier((own_rows[row], after))
        return lax.ppermute(row, "member", SWAP), after

    local_index = observation_index - lax.axis_index(SPACE) * (strip_rows * columns)
    mine = jnp.take(jnp.concatenate(rows, axis=1), local_index, axis=1, mode="clip")
    swapped = [swap(0, edge)[0]]
    theirs = lax.ppermute(mine, "member", SWAP)
    other, theirs = swap(1, theirs)
    swapped.append(other)
    mean = (jnp.sum(mine, axis=0) + jnp.sum(theirs, axis=0)) / members
    predicted = jnp.concatenate([mine, theirs], axis=0)
    anomalies = (predicted - mean[None, :]) / (observation_spread[None, :] * square_root_scale)
    innovations = (
        measured_values[None, :] + observation_spread[None, :] * observation_jitter - mine
    ) / observation_spread[None, :]
    stacked = jnp.concatenate([anomalies, innovations], axis=0)
    products = jnp.dot(
        anomalies, stacked.T, precision=HIGHEST, preferred_element_type=jnp.float32
    )
    whole, summed = reduce_over_space(products)
    for r in range(2, strip_rows):
        other, summed = swap(r, summed)
        swapped.append(other)
    mixing = solve(whole) / square_root_scale
    revised = [
        own_rows[r]
        + lax.dot_general(
            mixing,
            jnp.concatenate([own_rows[r], swapped[r]], axis=0),
            (((0,), (0,)), ((), ())),
            precision=HIGHEST,
            preferred_element_type=jnp.float32,
        )
        for r in range(strip_rows)
    ]
    return (jnp.stack(revised, axis=1), jnp.stack(rows, axis=1))


def solution(mesh):
    fine = Mesh(mesh.devices.reshape(2, 8, 4, 2, 2), ("member",) + SPACE)
    in_specs = (
        P("member", SPACE, None),
        P("member", SPACE, None),
        P(SPACE, None),
        P(),
        P(SPACE),
        P(SPACE),
        P(SPACE),
        P("member", SPACE),
    )
    out_specs = (P("member", SPACE, None), P("member", SPACE, None))
    return jax.shard_map(strip, mesh=fine, in_specs=in_specs, out_specs=out_specs, check_vma=False)
```

```python
import math

import jax
import jax.numpy as jnp
from jax import lax
from jax.experimental import pallas as pl
from jax.experimental.pallas import tpu as pltpu
from jax.sharding import Mesh, PartitionSpec as P

time_step = 0.06
SPACE = ("z", "y", "xh", "core")
CHIPS = ("z", "y", "xh")
SWAP = [(0, 1), (1, 0)]
HIGHEST = lax.Precision.HIGHEST
BLOCK = 64
PARTS = 2


def invert_block(block):
    size = block.shape[0]
    wide = 2 * size
    row_id = lax.broadcasted_iota(jnp.int32, (size, wide), 0)
    r = lax.broadcasted_iota(jnp.int32, (size, size), 0)
    c = lax.broadcasted_iota(jnp.int32, (size, size), 1)
    aug = jnp.concatenate([block, (r == c).astype(jnp.float32)], axis=1)
    for p in range(0, size, 4):
        cols = [jnp.broadcast_to(aug[:, p + i : p + i + 1], (size, wide)) for i in range(4)]
        rows = [aug[p + i : p + i + 1, :] for i in range(4)]
        e = [[cols[j][p + i : p + i + 1, :] for j in range(4)] for i in range(4)]
        a, b, d = e[0][0], e[1][0], e[1][1]
        inv = 1.0 / (a * d - b * b)
        t0 = (d * rows[0] - b * rows[1]) * inv
        t1 = (a * rows[1] - b * rows[0]) * inv
        u, v, w, x = e[2][0], e[2][1], e[3][0], e[3][1]
        l00 = (d * u - b * v) * inv
        l01 = (a * v - b * u) * inv
        l10 = (d * w - b * x) * inv
        l11 = (a * x - b * w) * inv
        sa = e[2][2] - (u * l00 + v * l01)
        sb = e[3][2] - (w * l00 + x * l01)
        sd = e[3][3] - (w * l10 + x * l11)
        s2 = rows[2] - (l00 * rows[0] + l01 * rows[1])
        s3 = rows[3] - (l10 * rows[0] + l11 * rows[1])
        sinv = 1.0 / (sa * sd - sb * sb)
        n2 = (sd * s2 - sb * s3) * sinv
        n3 = (sa * s3 - sb * s2) * sinv
        news = [t0 - (l00 * n2 + l10 * n3), t1 - (l01 * n2 + l11 * n3), n2, n3]
        out = aug
        for i in range(4):
            out = out - cols[i] * news[i]
        for i in range(4):
            out = jnp.where(row_id == p + i, news[i], out)
        aug = out
    return aug[:, size:]


def solve_kernel(g_ref, x_ref, w):
    m = g_ref.shape[0]
    w[...] = g_ref[...]
    r = lax.broadcasted_iota(jnp.int32, (m, m), 0)
    c = lax.broadcasted_iota(jnp.int32, (m, m), 1)
    w[:, :m] = w[:, :m] + (r == c).astype(jnp.float32)
    rows = lax.broadcasted_iota(jnp.int32, (m, 1), 0)
    for at in range(0, m, BLOCK):
        end = at + BLOCK
        lo = end // 128 * 128
        inv = invert_block(w[at:end, at:end])
        new = jnp.dot(inv, w[at:end, lo:], precision=HIGHEST, preferred_element_type=jnp.float32)
        left = jnp.where((rows >= at) & (rows < end), 0.0, w[:, at:end])
        w[:, lo:] = w[:, lo:] - jnp.dot(
            left, new, precision=HIGHEST, preferred_element_type=jnp.float32
        )
        w[at:end, lo:] = new
    x_ref[...] = w[:, m:]


def solve(system):
    m, wide = system.shape
    vmem = pl.BlockSpec(memory_space=pltpu.VMEM)
    return pl.pallas_call(
        solve_kernel,
        out_shape=jax.ShapeDtypeStruct((m, wide - m), jnp.float32),
        in_specs=[vmem],
        out_specs=vmem,
        scratch_shapes=[pltpu.VMEM((m, wide), jnp.float32)],
        cost_estimate=pl.CostEstimate(flops=200_000_000, bytes_accessed=600_000, transcendentals=0),
        name="solve",
    )(system)


def split_kernel(x_ref, *out_refs):
    for r, out_ref in enumerate(out_refs):
        out_ref[...] = x_ref[:, r, :]


def split_rows(x):
    m, rows, cols = x.shape
    return pl.pallas_call(
        split_kernel,
        grid=(PARTS,),
        out_shape=[jax.ShapeDtypeStruct((m, cols), jnp.float32)] * rows,
        in_specs=[pl.BlockSpec((m // PARTS, rows, cols), lambda i: (i, 0, 0))],
        out_specs=[pl.BlockSpec((m // PARTS, cols), lambda i: (i, 0))] * rows,
        cost_estimate=pl.CostEstimate(flops=0, bytes_accessed=8 * x.size, transcendentals=0),
        name="split_rows",
    )(x)


def merge_kernel(*refs):
    for r, x_ref in enumerate(refs[:-1]):
        refs[-1][:, r, :] = x_ref[...]


def merge_rows(rows):
    m, cols = rows[0].shape
    count = len(rows)
    return pl.pallas_call(
        merge_kernel,
        grid=(PARTS,),
        out_shape=jax.ShapeDtypeStruct((m, count, cols), jnp.float32),
        in_specs=[pl.BlockSpec((m // PARTS, cols), lambda i: (i, 0))] * count,
        out_specs=pl.BlockSpec((m // PARTS, count, cols), lambda i: (i, 0, 0)),
        cost_estimate=pl.CostEstimate(
            flops=0, bytes_accessed=8 * count * m * cols, transcendentals=0
        ),
        name="merge_rows",
    )(*rows)


def finish_kernel(mix_ref, own_ref, first_ref, second_ref, rest_ref, out_ref):
    m, rows, _ = own_ref.shape
    dims = (((0,), (0,)), ((), ()))
    mix = mix_ref[...] * (1.0 / math.sqrt(2 * m - 1))
    low, high = mix[:m, :], mix[m:, :]
    for r in range(rows):
        mine = own_ref[:, r, :]
        other = (first_ref, second_ref)[r][...] if r < 2 else rest_ref[r - 2]
        out_ref[:, r, :] = mine + (
            lax.dot_general(low, mine, dims, precision=HIGHEST, preferred_element_type=jnp.float32)
            + lax.dot_general(
                high, other, dims, precision=HIGHEST, preferred_element_type=jnp.float32
            )
        )


def finish(mixing, params, first, second, rest):
    m, rows, cols = params.shape
    piece = cols // PARTS
    flat = pl.BlockSpec((m, piece), lambda i: (0, i))
    whole = pl.BlockSpec((m, rows, piece), lambda i: (0, 0, i))
    return pl.pallas_call(
        finish_kernel,
        grid=(PARTS,),
        out_shape=jax.ShapeDtypeStruct((m, rows, cols), jnp.float32),
        in_specs=[
            pl.BlockSpec((2 * m, m), lambda i: (0, 0)),
            whole,
            flat,
            flat,
            pl.BlockSpec((rows - 2, m, piece), lambda i: (0, 0, i)),
        ],
        out_specs=whole,
        cost_estimate=pl.CostEstimate(
            flops=4 * m * m * rows * cols, bytes_accessed=12 * params.size, transcendentals=0
        ),
        name="finish",
    )(mixing, params, first, second, rest)


def coef_fields(regime, regime_coefs):
    levels = jnp.arange(regime_coefs.shape[0], dtype=jnp.int32)
    onehot = (regime[None, :, :] == levels[:, None, None]).astype(jnp.float32)
    return jnp.einsum("rd,rxy->dxy", regime_coefs, onehot, precision=lax.Precision.HIGHEST)


def halo(head, tail):
    ends = lax.axis_size(SPACE) - 1
    above = lax.ppermute(tail, SPACE, [(i, i + 1) for i in range(ends)])
    below = lax.ppermute(head, SPACE, [(i + 1, i) for i in range(ends)])
    return above, below


def advance(above, center, below, rate, coef):
    padded = jnp.pad(center, ((0, 0), (1, 1)))
    flow = coef[0] * (above - center) + coef[1] * (below - center)
    flow = flow + coef[2] * (padded[:, :-2] - center) + coef[3] * (padded[:, 2:] - center)
    return center + rate * flow


def two_steps(rows, rates, coefs):
    last = len(rows) - 1
    above, below = halo(rows[0], rows[last])
    for repeat in range(2):
        ends = (
            advance(above, rows[0], rows[1], rates[0], coefs[0]),
            advance(rows[last - 1], rows[last], below, rates[last], coefs[last]),
        )
        inner = [
            advance(rows[r - 1], rows[r], rows[r + 1], rates[r], coefs[r]) for r in range(1, last)
        ]
        if repeat == 0:
            ends = lax.optimization_barrier(ends)
            above, below = halo(*ends)
        rows = [ends[0], *inner, ends[1]]
    return rows, (above, below)


def reduce_over_space(block):
    half = block.shape[0] // 2
    core = lax.axis_index("core")
    low, high = block[:half], block[half:]
    first = core == 0
    kept = jnp.where(first, low, high)
    sent = jnp.where(first, high, low)
    part = kept + lax.ppermute(sent, "core", SWAP)
    chips = lax.axis_size(CHIPS)
    pieces = lax.all_to_all(part, CHIPS, 0, 0, tiled=True)
    piece = jnp.sum(pieces.reshape(chips, half // chips, -1), axis=0)
    spread = jnp.broadcast_to(piece[None], (chips,) + piece.shape).reshape(half, -1)
    summed = lax.all_to_all(spread, CHIPS, 0, 0, tiled=True)
    other = lax.ppermute(summed, "core", SWAP)
    whole = jnp.concatenate(
        [jnp.where(first, summed, other), jnp.where(first, other, summed)], axis=0
    )
    return whole, other


def strip(
    params,
    state,
    regime,
    regime_coefs,
    observation_index,
    measured_values,
    observation_spread,
    observation_jitter,
):
    own = params.shape[0]
    strip_rows = params.shape[1]
    columns = params.shape[2]
    members = own * lax.axis_size("member")
    square_root_scale = math.sqrt(members - 1)
    fields = coef_fields(regime, regime_coefs)
    coefs = [fields[:, r] for r in range(strip_rows)]
    by_row = lax.optimization_barrier(jnp.swapaxes(params, 0, 1))
    own_rows = [by_row[r] for r in range(strip_rows)]
    rates = [time_step * jnp.exp(row) for row in own_rows]
    rows, edge = two_steps(split_rows(state), rates, coefs)

    def swap(piece, after):
        piece, after = lax.optimization_barrier((piece, after))
        return lax.ppermute(piece, "member", SWAP), after

    local_index = observation_index - lax.axis_index(SPACE) * (strip_rows * columns)
    mine = jnp.take(jnp.concatenate(rows, axis=1), local_index, axis=1, mode="clip")
    first, _ = swap(own_rows[0], edge)
    predicted_state = merge_rows(rows)
    theirs = lax.ppermute(mine, "member", SWAP)
    second, theirs = swap(own_rows[1], theirs)
    mean = (jnp.sum(mine, axis=0) + jnp.sum(theirs, axis=0)) / members
    predicted = jnp.concatenate([mine, theirs], axis=0)
    anomalies = (predicted - mean[None, :]) / (observation_spread[None, :] * square_root_scale)
    innovations = (
        measured_values[None, :] + observation_spread[None, :] * observation_jitter - mine
    ) / observation_spread[None, :]
    stacked = jnp.concatenate([anomalies, innovations], axis=0)
    products = jnp.dot(
        anomalies, stacked.T, precision=HIGHEST, preferred_element_type=jnp.float32
    )
    whole, received = reduce_over_space(products)
    rest, _ = swap(by_row[2:], received)
    mixing = solve(whole)
    return (finish(mixing, params, first, second, rest), predicted_state)


def solution(mesh):
    fine = Mesh(mesh.devices.reshape(2, 8, 4, 2, 2), ("member",) + SPACE)
    in_specs = (
        P("member", SPACE, None),
        P("member", SPACE, None),
        P(SPACE, None),
        P(),
        P(SPACE),
        P(SPACE),
        P(SPACE),
        P("member", SPACE),
    )
    out_specs = (P("member", SPACE, None), P("member", SPACE, None))
    return jax.shard_map(strip, mesh=fine, in_specs=in_specs, out_specs=out_specs, check_vma=False)
```

```python
import math

import jax
import jax.numpy as jnp
from jax import lax
from jax.experimental import pallas as pl
from jax.experimental.pallas import tpu as pltpu
from jax.sharding import Mesh, PartitionSpec as P

time_step = 0.06
SPACE = ("z", "y", "xh", "core")
CHIPS = ("z", "y", "xh")
SWAP = [(0, 1), (1, 0)]
HIGHEST = lax.Precision.HIGHEST
BLOCK = 64
PARTS = 2


def invert_block(block):
    size = block.shape[0]
    wide = 2 * size
    row_id = lax.broadcasted_iota(jnp.int32, (size, wide), 0)
    r = lax.broadcasted_iota(jnp.int32, (size, size), 0)
    c = lax.broadcasted_iota(jnp.int32, (size, size), 1)
    aug = jnp.concatenate([block, (r == c).astype(jnp.float32)], axis=1)
    for p in range(0, size, 4):
        cols = [jnp.broadcast_to(aug[:, p + i : p + i + 1], (size, wide)) for i in range(4)]
        rows = [aug[p + i : p + i + 1, :] for i in range(4)]
        e = [[cols[j][p + i : p + i + 1, :] for j in range(4)] for i in range(4)]
        a, b, d = e[0][0], e[1][0], e[1][1]
        inv = 1.0 / (a * d - b * b)
        t0 = (d * rows[0] - b * rows[1]) * inv
        t1 = (a * rows[1] - b * rows[0]) * inv
        u, v, w, x = e[2][0], e[2][1], e[3][0], e[3][1]
        l00 = (d * u - b * v) * inv
        l01 = (a * v - b * u) * inv
        l10 = (d * w - b * x) * inv
        l11 = (a * x - b * w) * inv
        sa = e[2][2] - (u * l00 + v * l01)
        sb = e[3][2] - (w * l00 + x * l01)
        sd = e[3][3] - (w * l10 + x * l11)
        s2 = rows[2] - (l00 * rows[0] + l01 * rows[1])
        s3 = rows[3] - (l10 * rows[0] + l11 * rows[1])
        sinv = 1.0 / (sa * sd - sb * sb)
        n2 = (sd * s2 - sb * s3) * sinv
        n3 = (sa * s3 - sb * s2) * sinv
        news = [t0 - (l00 * n2 + l10 * n3), t1 - (l01 * n2 + l11 * n3), n2, n3]
        out = aug
        for i in range(4):
            out = out - cols[i] * news[i]
        for i in range(4):
            out = jnp.where(row_id == p + i, news[i], out)
        aug = out
    return aug[:, size:]


def solve_kernel(g_ref, x_ref, w):
    m = g_ref.shape[0]
    w[...] = g_ref[...]
    r = lax.broadcasted_iota(jnp.int32, (m, m), 0)
    c = lax.broadcasted_iota(jnp.int32, (m, m), 1)
    w[:, :m] = w[:, :m] + (r == c).astype(jnp.float32)
    rows = lax.broadcasted_iota(jnp.int32, (m, 1), 0)
    for at in range(0, m, BLOCK):
        end = at + BLOCK
        lo = end // 128 * 128
        inv = invert_block(w[at:end, at:end])
        new = jnp.dot(inv, w[at:end, lo:], precision=HIGHEST, preferred_element_type=jnp.float32)
        left = jnp.where((rows >= at) & (rows < end), 0.0, w[:, at:end])
        w[:, lo:] = w[:, lo:] - jnp.dot(
            left, new, precision=HIGHEST, preferred_element_type=jnp.float32
        )
        w[at:end, lo:] = new
    x_ref[...] = w[:, m:]


def solve(system):
    m, wide = system.shape
    vmem = pl.BlockSpec(memory_space=pltpu.VMEM)
    return pl.pallas_call(
        solve_kernel,
        out_shape=jax.ShapeDtypeStruct((m, wide - m), jnp.float32),
        in_specs=[vmem],
        out_specs=vmem,
        scratch_shapes=[pltpu.VMEM((m, wide), jnp.float32)],
        cost_estimate=pl.CostEstimate(flops=200_000_000, bytes_accessed=600_000, transcendentals=0),
        name="solve",
    )(system)


def split_kernel(x_ref, *out_refs):
    for r, out_ref in enumerate(out_refs):
        out_ref[...] = x_ref[:, r, :]


def split_rows(x):
    m, rows, cols = x.shape
    return pl.pallas_call(
        split_kernel,
        grid=(PARTS,),
        out_shape=[jax.ShapeDtypeStruct((m, cols), jnp.float32)] * rows,
        in_specs=[pl.BlockSpec((m // PARTS, rows, cols), lambda i: (i, 0, 0))],
        out_specs=[pl.BlockSpec((m // PARTS, cols), lambda i: (i, 0))] * rows,
        cost_estimate=pl.CostEstimate(flops=0, bytes_accessed=8 * x.size, transcendentals=0),
        name="split_rows",
    )(x)


def merge_kernel(*refs):
    for r, x_ref in enumerate(refs[:-1]):
        refs[-1][:, r, :] = x_ref[...]


def merge_rows(rows):
    m, cols = rows[0].shape
    count = len(rows)
    return pl.pallas_call(
        merge_kernel,
        grid=(PARTS,),
        out_shape=jax.ShapeDtypeStruct((m, count, cols), jnp.float32),
        in_specs=[pl.BlockSpec((m // PARTS, cols), lambda i: (i, 0))] * count,
        out_specs=pl.BlockSpec((m // PARTS, count, cols), lambda i: (i, 0, 0)),
        cost_estimate=pl.CostEstimate(
            flops=0, bytes_accessed=8 * count * m * cols, transcendentals=0
        ),
        name="merge_rows",
    )(*rows)


def finish_kernel(mix_ref, own_ref, first_ref, middle_ref, last_ref, out_ref):
    m, rows, _ = own_ref.shape
    dims = (((0,), (0,)), ((), ()))
    mix = mix_ref[...] * (1.0 / math.sqrt(2 * m - 1))
    low, high = mix[:m, :], mix[m:, :]
    for r in range(rows):
        mine = own_ref[:, r, :]
        if r == 0:
            other = first_ref[...]
        elif r == rows - 1:
            other = last_ref[...]
        else:
            other = middle_ref[r - 1]
        out_ref[:, r, :] = mine + (
            lax.dot_general(low, mine, dims, precision=HIGHEST, preferred_element_type=jnp.float32)
            + lax.dot_general(
                high, other, dims, precision=HIGHEST, preferred_element_type=jnp.float32
            )
        )


def finish(mixing, params, first, middle, last):
    m, rows, cols = params.shape
    piece = cols // PARTS
    flat = pl.BlockSpec((m, piece), lambda i: (0, i))
    whole = pl.BlockSpec((m, rows, piece), lambda i: (0, 0, i))
    return pl.pallas_call(
        finish_kernel,
        grid=(PARTS,),
        out_shape=jax.ShapeDtypeStruct((m, rows, cols), jnp.float32),
        in_specs=[
            pl.BlockSpec((2 * m, m), lambda i: (0, 0)),
            whole,
            flat,
            pl.BlockSpec((rows - 2, m, piece), lambda i: (0, 0, i)),
            flat,
        ],
        out_specs=whole,
        cost_estimate=pl.CostEstimate(
            flops=4 * m * m * rows * cols, bytes_accessed=12 * params.size, transcendentals=0
        ),
        name="finish",
    )(mixing, params, first, middle, last)


def coef_fields(regime, regime_coefs):
    levels = jnp.arange(regime_coefs.shape[0], dtype=jnp.int32)
    onehot = (regime[None, :, :] == levels[:, None, None]).astype(jnp.float32)
    return jnp.einsum("rd,rxy->dxy", regime_coefs, onehot, precision=lax.Precision.HIGHEST)


def halo(head, tail):
    ends = lax.axis_size(SPACE) - 1
    above = lax.ppermute(tail, SPACE, [(i, i + 1) for i in range(ends)])
    below = lax.ppermute(head, SPACE, [(i + 1, i) for i in range(ends)])
    return above, below


def advance(above, center, below, rate, coef):
    padded = jnp.pad(center, ((0, 0), (1, 1)))
    flow = coef[0] * (above - center) + coef[1] * (below - center)
    flow = flow + coef[2] * (padded[:, :-2] - center) + coef[3] * (padded[:, 2:] - center)
    return center + rate * flow


def two_steps(rows, rates, coefs):
    last = len(rows) - 1
    above, below = halo(rows[0], rows[last])
    for repeat in range(2):
        ends = (
            advance(above, rows[0], rows[1], rates[0], coefs[0]),
            advance(rows[last - 1], rows[last], below, rates[last], coefs[last]),
        )
        inner = [
            advance(rows[r - 1], rows[r], rows[r + 1], rates[r], coefs[r]) for r in range(1, last)
        ]
        if repeat == 0:
            ends = lax.optimization_barrier(ends)
            above, below = halo(*ends)
        rows = [ends[0], *inner, ends[1]]
    return rows, (above, below)


def reduce_over_space(block):
    half = block.shape[0] // 2
    core = lax.axis_index("core")
    low, high = block[:half], block[half:]
    first = core == 0
    kept = jnp.where(first, low, high)
    sent = jnp.where(first, high, low)
    part = kept + lax.ppermute(sent, "core", SWAP)
    chips = lax.axis_size(CHIPS)
    pieces = lax.all_to_all(part, CHIPS, 0, 0, tiled=True)
    piece = jnp.sum(pieces.reshape(chips, half // chips, -1), axis=0)
    spread = jnp.broadcast_to(piece[None], (chips,) + piece.shape).reshape(half, -1)
    summed = lax.all_to_all(spread, CHIPS, 0, 0, tiled=True)
    other = lax.ppermute(summed, "core", SWAP)
    whole = jnp.concatenate(
        [jnp.where(first, summed, other), jnp.where(first, other, summed)], axis=0
    )
    return whole, other


def strip(
    params,
    state,
    regime,
    regime_coefs,
    observation_index,
    measured_values,
    observation_spread,
    observation_jitter,
):
    own = params.shape[0]
    strip_rows = params.shape[1]
    columns = params.shape[2]
    members = own * lax.axis_size("member")
    square_root_scale = math.sqrt(members - 1)
    fields = coef_fields(regime, regime_coefs)
    coefs = [fields[:, r] for r in range(strip_rows)]
    by_row = lax.optimization_barrier(jnp.swapaxes(params, 0, 1))
    own_rows = [by_row[r] for r in range(strip_rows)]
    rates = [time_step * jnp.exp(row) for row in own_rows]
    rows, edge = two_steps(split_rows(state), rates, coefs)

    def swap(piece, after):
        piece, after = lax.optimization_barrier((piece, after))
        return lax.ppermute(piece, "member", SWAP), after

    local_index = observation_index - lax.axis_index(SPACE) * (strip_rows * columns)
    mine = jnp.take(jnp.concatenate(rows, axis=1), local_index, axis=1, mode="clip")
    first, _ = swap(own_rows[0], edge)
    predicted_state = merge_rows(rows)
    theirs = lax.ppermute(mine, "member", SWAP)
    middle, theirs = swap(by_row[1:3], theirs)
    mean = (jnp.sum(mine, axis=0) + jnp.sum(theirs, axis=0)) / members
    predicted = jnp.concatenate([mine, theirs], axis=0)
    anomalies = (predicted - mean[None, :]) / (observation_spread[None, :] * square_root_scale)
    innovations = (
        measured_values[None, :] + observation_spread[None, :] * observation_jitter - mine
    ) / observation_spread[None, :]
    stacked = jnp.concatenate([anomalies, innovations], axis=0)
    products = jnp.dot(
        anomalies, stacked.T, precision=HIGHEST, preferred_element_type=jnp.float32
    )
    whole, received = reduce_over_space(products)
    last, _ = swap(own_rows[3], received)
    mixing = solve(whole)
    return (finish(mixing, params, first, middle, last), predicted_state)


def solution(mesh):
    fine = Mesh(mesh.devices.reshape(2, 8, 4, 2, 2), ("member",) + SPACE)
    in_specs = (
        P("member", SPACE, None),
        P("member", SPACE, None),
        P(SPACE, None),
        P(),
        P(SPACE),
        P(SPACE),
        P(SPACE),
        P("member", SPACE),
    )
    out_specs = (P("member", SPACE, None), P("member", SPACE, None))
    return jax.shard_map(strip, mesh=fine, in_specs=in_specs, out_specs=out_specs, check_vma=False)
```
